32 devices in a mesh: dom: 4 (over z), elem: 8 (over y, x, core).
Axes of the slice: x: 2, y: 2, z: 4, core: 2. Of those that a mesh axis runs over, the one named last changes fastest.
Arguments:
- positions: float32 [2048, 3, 128], P(('dom', 'elem')), may hold values from -6 to 6
- velocities: float32 [2048, 3, 128], P(('dom', 'elem')), may hold values from -6 to 6
- inv_mass: float32 [2048, 128], P(('dom', 'elem')), may hold values from 0.25 to 2
- send_index: int32 [32, 32, 4], P(('dom', 'elem')), may hold values from 0 to 63
- pair_slave: int32 [32, 128], P(('dom', 'elem')), may hold values from 0 to 63
- pair_live: int32 [32, 128], P(('dom', 'elem')), may hold values from 0 to 1, as said below
- quad_weights: float32 [32, 128, 128], P(('dom', 'elem')), may hold values from 0.25 to 2
- seg_normals: float32 [32, 128, 3, 128], P(('dom', 'elem')), may hold values from -6 to 6
- slave_shape: float32 [128, 128], replicated, may hold values from -0.5 to 0.5
- master_shape: float32 [128, 128], replicated, may hold values from -0.5 to 0.5
- stiffness: float32 [128, 128], replicated, may hold values from -0.5 to 0.5
Outputs:
- velocity_new: float32 [2048, 3, 128], P(('dom', 'elem'))
- contact: float32 [2048, 3, 128], P(('dom', 'elem'))
The draws below stay inside these ranges and needn't reach their ends.
Inputs may be any that keep to these rules, and one draw needn't show every extreme that they name: `pair_live`: at least one device has all 128 pair slots live; the share of live slots differs from device to device.
All inputs are finite; a program needn't handle non-finite values.
Results may differ from the reference program's by a relative error of at most 0.0003.
Values sent between devices are 32-bit elements; how exact they have to be, the bound alone decides.
No kernel may reach another device: no remote copies, remote signals or barrier semaphores. Data moves between devices by JAX's collectives and lax.ppermute only.
A program may use at most 64 MiB of HBM per device.

```python
import math
import jax
import jax.numpy as jnp
from jax import lax

NODES = 128
SEG = 128
PATCH_DEV = 64
SLOTS = 4
PAIRS_DEV = 128
PATCHES = 2048
N_DOM = 4
N_ELEM = 8
DEVICES = 32


def draw_pair_live(key, part):
    first, second, third = jax.random.split(jax.random.fold_in(key, 71), 3)
    shares = jax.random.randint(first, (DEVICES, 1), 20, 101)
    filled = jax.random.randint(second, (), 0, DEVICES)
    shares = jnp.where(jnp.arange(DEVICES)[:, None] == filled, 100, shares)
    rolled = jax.random.randint(third, (DEVICES, PAIRS_DEV), 0, 100)
    return (rolled < shares).astype(jnp.int32)


def touch_ends(drawn, stream_key, low, top_value):
    dims = drawn.shape
    spot = [jax.random.randint(jax.random.fold_in(stream_key, axis), (), 0, dims[axis]) for axis in range(len(dims))]
    drawn = drawn.at[tuple(spot)].set(low)
    longest = dims.index(max(dims))
    spot[longest] = (spot[longest] + 1) % dims[longest]
    return drawn.at[tuple(spot)].set(top_value)


def shard_levels(key, shape, shards, least, high):
    def one(position, blocks):
        draws = jax.random.uniform(jax.random.fold_in(jax.random.fold_in(key, 6), position), (blocks,), jnp.float32, least / len(shards), high / len(shards))
        return jnp.repeat(jnp.exp(draws), shape[position] // blocks).reshape((-1,) + (1,) * (len(shape) - position - 1))

    level = one(*shards[0])
    for cut in shards[1:]:
        level = level * one(*cut)
    return level


def noise(own_key, extent, deviation, reach, pieces=(), held_as=jnp.bfloat16):
    array = deviation * jax.random.normal(own_key, extent, jnp.float32)
    if pieces:
        array = array * shard_levels(own_key, extent, pieces, -0.22, 0.18)
    return jnp.clip(array, -reach, reach).astype(held_as)


def setup_inputs(seed: int = 0) -> dict:
    streams_of = jax.random.split(jax.random.key(seed), 12)
    positions = noise(streams_of[0], (PATCHES, 3, NODES), 1.0, 6.0, ((0, 32),), jnp.float32)
    velocities = noise(streams_of[1], (PATCHES, 3, NODES), 1.0, 6.0, ((0, 32),), jnp.float32)
    inv_mass = jnp.clip(jnp.exp(math.log(2.0) - 2.0794415 * jax.random.uniform(streams_of[2], (PATCHES, NODES), jnp.float32) ** shard_levels(streams_of[2], (PATCHES, NODES), ((0, 32),), -0.2, 0.2)), 0.25, 2.0)
    send_index = touch_ends(jax.random.randint(streams_of[3], (DEVICES, DEVICES, SLOTS), 0, PATCH_DEV), jax.random.fold_in(streams_of[3], 1), 0, PATCH_DEV - 1).astype(jnp.int32)
    pair_slave = touch_ends(jax.random.randint(streams_of[4], (DEVICES, PAIRS_DEV), 0, PATCH_DEV), jax.random.fold_in(streams_of[4], 1), 0, PATCH_DEV - 1).astype(jnp.int32)
    pair_live = draw_pair_live(jax.random.fold_in(streams_of[11], 71), 0)
    quad_weights = jnp.clip(jnp.exp(math.log(2.0) - 2.0794415 * jax.random.uniform(streams_of[6], (DEVICES, PAIRS_DEV, SEG), jnp.float32) ** shard_levels(streams_of[6], (DEVICES, PAIRS_DEV, SEG), ((0, 32),), -0.2, 0.2)), 0.25, 2.0)
    seg_normals = noise(streams_of[7], (DEVICES, PAIRS_DEV, 3, SEG), 1.0, 6.0, ((0, 32),), jnp.float32)
    slave_shape = noise(streams_of[8], (NODES, SEG), NODES ** -0.5, 0.5, (), jnp.float32)
    master_shape = noise(streams_of[9], (NODES, SEG), NODES ** -0.5, 0.5, (), jnp.float32)
    stiffness = noise(streams_of[10], (NODES, NODES), NODES ** -0.5, 0.5, (), jnp.float32)
    return dict(positions=positions, velocities=velocities, inv_mass=inv_mass, send_index=send_index, pair_slave=pair_slave, pair_live=pair_live, quad_weights=quad_weights, seg_normals=seg_normals, slave_shape=slave_shape, master_shape=master_shape, stiffness=stiffness)


HIGH = lax.Precision.HIGHEST


def pair_forces(slave_states, master_states, live, weights, normals, slave_shape, master_shape):
    count = slave_states.shape[0]
    slave_proj = jnp.dot(slave_states.reshape(count * 6, -1), slave_shape, precision=HIGH).reshape(count, 6, -1)
    master_proj = jnp.dot(master_states.reshape(count * 6, -1), master_shape, precision=HIGH).reshape(count, 6, -1)
    gap_vector = slave_proj[:, :3] - master_proj[:, :3]
    gap_rate = slave_proj[:, 3:] - master_proj[:, 3:]
    normal_gap = jnp.sum(normals * gap_vector, axis=1)
    normal_rate = jnp.sum(normals * gap_rate, axis=1)
    pressure = jax.nn.softplus(-(normal_gap + 0.5 * normal_rate)) * weights * live.astype(jnp.float32)[:, None]
    traction = (normals * pressure[:, None, :]).reshape(count * 3, -1)
    slave_force = jnp.dot(traction, slave_shape.T, precision=HIGH).reshape(count, 3, -1)
    master_force = -jnp.dot(traction, master_shape.T, precision=HIGH).reshape(count, 3, -1)
    return slave_force, master_force


def reference(positions, velocities, inv_mass, send_index, pair_slave, pair_live, quad_weights, seg_normals, slave_shape, master_shape, stiffness):
    states = jnp.concatenate([positions, velocities], axis=1)
    offsets = jnp.arange(DEVICES, dtype=jnp.int32)[:, None] * PATCH_DEV

    def per_device(index):
        master_index = (offsets + send_index[:, index, :]).reshape(-1).astype(jnp.int32)
        slave_index = (index * PATCH_DEV + pair_slave[index]).astype(jnp.int32)
        slave_force, master_force = pair_forces(states[slave_index], states[master_index], pair_live[index], quad_weights[index], seg_normals[index], slave_shape, master_shape)
        return slave_force, master_force, slave_index, master_index

    slave_force, master_force, slave_all, master_all = lax.map(per_device, jnp.arange(DEVICES, dtype=jnp.int32))
    contact = jnp.zeros((PATCHES, 3, NODES), jnp.float32)
    contact = contact.at[slave_all.reshape(-1)].add(slave_force.reshape(-1, 3, NODES))
    contact = contact.at[master_all.reshape(-1)].add(master_force.reshape(-1, 3, NODES))
    chain = positions.reshape(N_DOM, N_ELEM * PATCH_DEV, 3, NODES)
    padded = jnp.pad(chain, ((0, 0), (1, 1), (0, 0), (0, 0)))
    neighbour = (padded[:, :-2] + padded[:, 2:] - 2.0 * chain).reshape(PATCHES, 3, NODES)
    internal = -jnp.dot(positions.reshape(-1, NODES), stiffness, precision=HIGH).reshape(PATCHES, 3, NODES) + 0.5 * neighbour
    velocity_new = velocities + 0.5 * inv_mass[:, None, :] * (internal + contact)
    return velocity_new, contact
```

```python
import functools

import jax
import jax.numpy as jnp
from jax import lax
from jax.experimental import pallas as pl
from jax.experimental.pallas import tpu as pltpu
from jax.sharding import PartitionSpec as P

VMEM = pl.BlockSpec(memory_space=pltpu.VMEM)
NN = (((1,), (0,)), ((), ()))
NT = (((1,), (1,)), ((), ()))
TN = (((0,), (0,)), ((), ()))


def split(x):
    high = x.astype(jnp.bfloat16)
    return high, (x - high.astype(jnp.float32)).astype(jnp.bfloat16)


def dot3(a, b, dims):
    a_high, a_low = split(a)
    b_high, b_low = split(b)
    dot = functools.partial(lax.dot_general, dimension_numbers=dims, preferred_element_type=jnp.float32)
    return dot(a_high, b_high) + (dot(a_high, b_low) + dot(a_low, b_high))


def pick(table, b, dims):
    high, low = split(b)
    dot = functools.partial(lax.dot_general, dimension_numbers=dims, preferred_element_type=jnp.float32)
    return dot(table, high) + dot(table, low)


def index_row(send_ref, slave_ref, patches):
    slots, peers = send_ref.shape
    width = 2 * slots
    columns = peers * width
    column = lax.broadcasted_iota(jnp.int32, (peers, columns), 1)
    peer = lax.broadcasted_iota(jnp.int32, (peers, columns), 0)
    spread = (column // width == peer).astype(jnp.bfloat16)
    masters = jnp.dot(send_ref[...].astype(jnp.bfloat16), spread, preferred_element_type=jnp.float32)
    slot = lax.broadcasted_iota(jnp.int32, (slots, columns), 0)
    place = lax.broadcasted_iota(jnp.int32, (slots, columns), 1) % width
    masters = jnp.sum(jnp.where(place == slot, masters, 0.0), axis=0, keepdims=True)
    pairs = peers * slots
    column = lax.broadcasted_iota(jnp.int32, (pairs, columns), 1)
    pair = lax.broadcasted_iota(jnp.int32, (pairs, columns), 0)
    spread = (column // width * slots + column % width - slots == pair) & (column % width >= slots)
    slaves = (slave_ref[...] + patches).astype(jnp.bfloat16)
    slaves = jnp.dot(slaves, spread.astype(jnp.bfloat16), preferred_element_type=jnp.float32)
    return (masters + slaves).astype(jnp.int32)


def table_of(row, patches):
    return (lax.broadcasted_iota(jnp.int32, (2 * patches, row.shape[1]), 0) == row).astype(jnp.bfloat16)


def pack_kernel(position_ref, velocity_ref, send_ref, slave_ref, live_ref, weight_ref, normal_ref, slave_shape_ref, master_shape_ref, out_ref):
    _, patches, nodes = position_ref.shape
    slots, peers = send_ref.shape
    segments = weight_ref.shape[-1]
    state = (position_ref[...] + 0.5 * velocity_ref[...]).reshape(3 * patches, nodes)
    master = dot3(state, master_shape_ref[...], NN).reshape(3, patches, segments)
    slave = dot3(state, slave_shape_ref[...], NN).reshape(3, patches, segments)
    table = table_of(index_row(send_ref, slave_ref, patches), patches)
    width = 2 * slots
    first = lax.broadcasted_iota(jnp.int32, (peers, width, segments), 1) < slots
    gap = jnp.zeros((peers, width, segments), jnp.float32)
    for c in range(3):
        both = jnp.concatenate([master[c], slave[c]], axis=0)
        picked = pick(table, both, TN).reshape(peers, width, segments)
        normal = normal_ref[c].reshape(peers, slots, segments)
        normal = jnp.concatenate([normal, normal], axis=1)
        gap = gap + normal * picked
        out_ref[:, c * width : (c + 1) * width, :] = jnp.where(first, picked, normal)
    live = live_ref[...].astype(jnp.float32).reshape(segments_of(live_ref), 1)
    weight = (weight_ref[...] * live).reshape(peers, slots, segments)
    weight = jnp.concatenate([weight, weight], axis=1)
    out_ref[:, 3 * width : 4 * width, :] = jnp.where(first, weight, gap)


def segments_of(ref):
    return ref.shape[1]


def chain_kernel(position_ref, velocity_ref, before_ref, after_ref, mass_ref, stiffness_ref, out_ref):
    _, patches, nodes = position_ref.shape
    position = position_ref[...]
    row = lax.broadcasted_iota(jnp.int32, (patches, nodes), 0)
    product = dot3(position.reshape(3 * patches, nodes), stiffness_ref[...], NN).reshape(3, patches, nodes)
    half = 0.5 * mass_ref[...]
    for c in range(3):
        x = position[c]
        before = jnp.where(row == 0, before_ref[c], pltpu.roll(x, 1, 0))
        after = jnp.where(row == patches - 1, after_ref[c], pltpu.roll(x, patches - 1, 0))
        internal = 0.5 * (before + after - 2.0 * x) - product[c]
        out_ref[c] = velocity_ref[c] + half * internal


def force_kernel(sent_ref, got_ref, send_ref, slave_ref, base_ref, mass_ref, slave_shape_ref, master_shape_ref, velocity_ref, contact_ref):
    _, patches, nodes = base_ref.shape
    slots, peers = send_ref.shape
    segments = sent_ref.shape[-1]
    width = 2 * slots
    first = lax.broadcasted_iota(jnp.int32, (peers, width, segments), 1) < slots
    table = table_of(index_row(send_ref, slave_ref, patches), patches)

    def swapped(x):
        return jnp.concatenate([x[:, slots:], x[:, :slots]], axis=1)

    normals = []
    gap = jnp.zeros((peers, width, segments), jnp.float32)
    for c in range(3):
        sent = sent_ref[:, c * width : (c + 1) * width, :]
        got = swapped(got_ref[:, c * width : (c + 1) * width, :])
        gap = gap - sent * got
        normals.append(jnp.where(first, got, sent))
    sent = sent_ref[:, 3 * width : 4 * width, :]
    got = got_ref[:, 3 * width : 4 * width, :]
    gap = gap + jnp.where(first, swapped(got), sent)
    weight = jnp.where(first, got, swapped(sent))
    pressure = (jnp.maximum(-gap, 0.0) + jnp.log1p(jnp.exp(-jnp.abs(gap)))) * weight
    half = 0.5 * mass_ref[...]
    for c in range(3):
        traction = (normals[c] * pressure).reshape(peers * width, segments)
        summed = pick(table, traction, NN)
        contact = dot3(summed[patches:], slave_shape_ref[...], NT) - dot3(summed[:patches], master_shape_ref[...], NT)
        contact_ref[c] = contact
        velocity_ref[c] = base_ref[c] + half * contact


def on_device(
    positions,
    velocities,
    inv_mass,
    send_index,
    pair_slave,
    pair_live,
    quad_weights,
    seg_normals,
    slave_shape,
    master_shape,
    stiffness,
):
    patches, _, nodes = positions.shape
    _, peers, slots = send_index.shape
    segments = quad_weights.shape[-1]
    place = jnp.transpose(positions, (1, 0, 2))
    speed = jnp.transpose(velocities, (1, 0, 2))
    send = jnp.transpose(send_index[0], (1, 0))
    normals = jnp.transpose(seg_normals[0], (1, 0, 2))
    sent = pl.pallas_call(
        pack_kernel,
        out_shape=jax.ShapeDtypeStruct((peers, 8 * slots, segments), jnp.float32),
        in_specs=[VMEM] * 9,
        out_specs=VMEM,
    )(place, speed, send, pair_slave, pair_live, quad_weights[0], normals, slave_shape, master_shape)
    got = lax.all_to_all(sent, ("dom", "elem"), split_axis=0, concat_axis=0, tiled=True)
    count = lax.axis_size("elem")
    before = lax.ppermute(place[:, -1:], "elem", [(i, i + 1) for i in range(count - 1)])
    after = lax.ppermute(place[:, :1], "elem", [(i + 1, i) for i in range(count - 1)])
    base = pl.pallas_call(
        chain_kernel,
        out_shape=jax.ShapeDtypeStruct((3, patches, nodes), jnp.float32),
        in_specs=[VMEM] * 6,
        out_specs=VMEM,
        cost_estimate=pl.CostEstimate(flops=6 * 3 * patches * nodes * nodes, bytes_accessed=16 * 3 * patches * nodes, transcendentals=0),
    )(place, speed, before, after, inv_mass, stiffness)
    velocity, contact = pl.pallas_call(
        force_kernel,
        out_shape=[jax.ShapeDtypeStruct((3, patches, nodes), jnp.float32)] * 2,
        in_specs=[VMEM] * 8,
        out_specs=[VMEM] * 2,
    )(sent, got, send, pair_slave, base, inv_mass, slave_shape, master_shape)
    return jnp.transpose(velocity, (1, 0, 2)), jnp.transpose(contact, (1, 0, 2))


def solution(mesh):
    both = ("dom", "elem")
    placed = (
        P(both, None, None),
        P(both, None, None),
        P(both, None),
        P(both, None, None),
        P(both, None),
        P(both, None),
        P(both, None, None),
        P(both, None, None, None),
        P(),
        P(),
        P(),
    )
    return jax.shard_map(
        on_device,
        mesh=mesh,
        in_specs=placed,
        out_specs=(P(both, None, None), P(both, None, None)),
        check_vma=False,
    )
```

```python
import functools

import jax
import jax.numpy as jnp
from jax import lax
from jax.experimental import pallas as pl
from jax.experimental.pallas import tpu as pltpu
from jax.sharding import PartitionSpec as P

VMEM = pl.BlockSpec(memory_space=pltpu.VMEM)
HBM = pl.BlockSpec(memory_space=pltpu.HBM)
SMALL = pltpu.CompilerParams(vmem_limit_bytes=16 << 20)
EXCHANGE = ("elem", "dom")
NN = (((1,), (0,)), ((), ()))
NT = (((1,), (1,)), ((), ()))
TN = (((0,), (0,)), ((), ()))


def dot(a, b, dims):
    return lax.dot_general(a, b, dims, preferred_element_type=jnp.float32)


def split(x):
    high = x.astype(jnp.bfloat16)
    return high, (x - high.astype(jnp.float32)).astype(jnp.bfloat16)


def dot3(a, b, dims):
    a_high, a_low = split(a)
    b_high, b_low = split(b)
    return dot(a_high, b_high, dims) + (dot(a_high, b_low, dims) + dot(a_low, b_high, dims))


def exchange_order():
    sizes = {"dom": lax.axis_size("dom"), "elem": lax.axis_size("elem")}
    assert EXCHANGE == ("elem", "dom")
    return [d * sizes["elem"] + e for e in range(sizes["elem"]) for d in range(sizes["dom"])]


def index_table(send, slave, patches, order):
    slots, peers = send.shape
    width = 2 * slots
    columns = peers * width
    outer = lax.axis_size(EXCHANGE[0])
    inner = lax.axis_size(EXCHANGE[1])

    def spot(peer):
        return peer % outer * inner + peer // outer

    column = lax.broadcasted_iota(jnp.int32, (peers, columns), 1)
    peer = lax.broadcasted_iota(jnp.int32, (peers, columns), 0)
    spread = (column // width == spot(peer)).astype(jnp.bfloat16)
    masters = dot(send.astype(jnp.bfloat16), spread, NN)
    slot = lax.broadcasted_iota(jnp.int32, (slots, columns), 0)
    place = lax.broadcasted_iota(jnp.int32, (slots, columns), 1) % width
    masters = jnp.sum(jnp.where(place == slot, masters, 0.0), axis=0, keepdims=True)
    pairs = peers * slots
    column = lax.broadcasted_iota(jnp.int32, (pairs, columns), 1)
    pair = lax.broadcasted_iota(jnp.int32, (pairs, columns), 0)
    spread = column == spot(pair // slots) * width + slots + pair % slots
    slaves = dot((slave + patches).astype(jnp.bfloat16), spread.astype(jnp.bfloat16), NN)
    row = (masters + slaves).astype(jnp.int32)
    return (lax.broadcasted_iota(jnp.int32, (2 * patches, columns), 0) == row).astype(jnp.bfloat16)


def pack_kernel(order, *refs):
    ins, out_hbm, vmem, packed, in_sems, out_sems = refs[:9], refs[9], refs[10:19], refs[19], refs[20], refs[21]
    loads = [pltpu.make_async_copy(ins[i], vmem[i], in_sems.at[i]) for i in range(9)]
    for load in loads:
        load.start()
    send_ref, slave_ref, position_ref, velocity_ref, master_ref, slave_shape_ref, normal_ref, weight_ref, live_ref = vmem
    _, patches, nodes = position_ref.shape
    slots, peers = send_ref.shape
    segments = weight_ref.shape[-1]
    width = 2 * slots
    loads[0].wait()
    loads[1].wait()
    table = index_table(send_ref[...], slave_ref[...], patches, order)
    for i in (2, 3, 4, 5):
        loads[i].wait()
    state = (position_ref[...] + 0.5 * velocity_ref[...]).reshape(3 * patches, nodes)
    shapes = jnp.concatenate([master_ref[...], slave_shape_ref[...]], axis=1)
    projected = dot3(state, shapes, NN).reshape(3, patches, 2 * segments)
    first = lax.broadcasted_iota(jnp.int32, (peers, width, segments), 1) < slots
    gap = jnp.zeros((peers, width, segments), jnp.float32)

    def ordered(x):
        x = x.reshape(peers, slots, segments)
        x = jnp.concatenate([x[p : p + 1] for p in order], axis=0)
        return jnp.concatenate([x, x], axis=1)

    stores = [
        pltpu.make_async_copy(packed.at[:, pl.ds(t * width, width), :], out_hbm.at[:, pl.ds(t * width, width), :], out_sems.at[t])
        for t in range(4)
    ]
    loads[6].wait()
    for c in range(3):
        both = jnp.concatenate([projected[c, :, :segments], projected[c, :, segments:]], axis=0)
        high, low = split(both)
        picked = (dot(table, high, TN) + dot(table, low, TN)).reshape(peers, width, segments)
        normal = ordered(normal_ref[c])
        gap = gap + normal * picked
        packed[:, c * width : (c + 1) * width, :] = jnp.where(first, picked, normal)
        stores[c].start()
    loads[7].wait()
    loads[8].wait()
    live = live_ref[...].astype(jnp.float32).reshape(peers * slots, 1)
    packed[:, 3 * width : 4 * width, :] = jnp.where(first, ordered(weight_ref[...] * live), gap)
    stores[3].start()
    for store in stores:
        store.wait()


def window_kernel(
    order,
    sent_ref, send_ref, slave_ref, position_ref, velocity_ref, before_ref, after_ref, mass_ref, stiffness_ref, slave_shape_ref, master_shape_ref,
    own_ref, table_ref, high_ref, low_ref, base_ref, half_ref,
):
    _, patches, nodes = position_ref.shape
    slots, peers = send_ref.shape
    width = 2 * slots
    own_ref[:, : 4 * width, :] = sent_ref[...]
    last = sent_ref[:, 3 * width : 4 * width, :]
    own_ref[:, 4 * width :, :] = pltpu.roll(last, slots, 1)
    table_ref[...] = index_table(send_ref[...], slave_ref[...], patches, order)
    high, low = split(jnp.concatenate([-master_shape_ref[...], slave_shape_ref[...]], axis=1))
    high_ref[...] = high
    low_ref[...] = low
    row = lax.broadcasted_iota(jnp.int32, (patches, nodes), 0)
    position = position_ref[...]
    product = dot3(position.reshape(3 * patches, nodes), stiffness_ref[...], NN).reshape(3, patches, nodes)
    half = 0.5 * mass_ref[...]
    half_ref[...] = half
    for c in range(3):
        x = position[c]
        before = jnp.where(row == 0, before_ref[c], pltpu.roll(x, 1, 0))
        after = jnp.where(row == patches - 1, after_ref[c], pltpu.roll(x, patches - 1, 0))
        internal = 0.5 * (before + after - 2.0 * x) - product[c]
        base_ref[c] = velocity_ref[c] + half * internal


def force_kernel(got_ref, own_ref, table_ref, shape_high_ref, shape_low_ref, base_ref, half_ref, velocity_ref, contact_ref, high_ref, low_ref):
    _, patches, nodes = base_ref.shape
    peers = got_ref.shape[0]
    segments = got_ref.shape[-1]
    width = got_ref.shape[1] // 4
    slots = width // 2
    group = 8
    first = lax.broadcasted_iota(jnp.int32, (group, width, segments), 1) < slots
    for g in range(0, peers, group):
        def own(t):
            return own_ref[g : g + group, t * width : (t + 1) * width, :]

        def got(t):
            return got_ref[g : g + group, t * width : (t + 1) * width, :]

        gap = jnp.where(first, pltpu.roll(got(3), slots, 1), own(3))
        weight = jnp.where(first, got(3), own(4))
        normals = []
        for c in range(3):
            mine = own(c)
            theirs = pltpu.roll(got(c), slots, 1)
            gap = gap - mine * theirs
            normals.append(jnp.where(first, theirs, mine))
        pressure = (jnp.maximum(-gap, 0.0) + jnp.log1p(jnp.exp(-jnp.abs(gap)))) * weight
        for c in range(3):
            high, low = split((normals[c] * pressure).reshape(group * width, segments))
            high_ref[g * width : (g + group) * width, c * segments : (c + 1) * segments] = high
            low_ref[g * width : (g + group) * width, c * segments : (c + 1) * segments] = low
    table = table_ref[...]
    summed = dot(table, high_ref[...], NN) + dot(table, low_ref[...], NN)
    summed = jnp.concatenate(
        [
            jnp.concatenate([summed[:patches, c * segments : (c + 1) * segments], summed[patches:, c * segments : (c + 1) * segments]], axis=1)
            for c in range(3)
        ],
        axis=0,
    )
    high, low = split(summed)
    contact = dot(high, shape_high_ref[...], NT) + (dot(high, shape_low_ref[...], NT) + dot(low, shape_high_ref[...], NT))
    contact = contact.reshape(3, patches, nodes)
    contact_ref[...] = contact
    velocity_ref[...] = base_ref[...] + half_ref[...] * contact


def on_device(
    positions,
    velocities,
    inv_mass,
    send_index,
    pair_slave,
    pair_live,
    quad_weights,
    seg_normals,
    slave_shape,
    master_shape,
    stiffness,
):
    patches, _, nodes = positions.shape
    _, peers, slots = send_index.shape
    segments = quad_weights.shape[-1]
    rows = 8 * slots
    f32, bf16 = jnp.float32, jnp.bfloat16
    order = exchange_order()
    place = jnp.transpose(positions, (1, 0, 2))
    speed = jnp.transpose(velocities, (1, 0, 2))
    send = jnp.transpose(send_index[0], (1, 0))
    normals = jnp.transpose(seg_normals[0], (1, 0, 2))
    operands = (send, pair_slave, place, speed, master_shape, slave_shape, normals, quad_weights[0], pair_live)
    sent = pl.pallas_call(
        functools.partial(pack_kernel, order),
        out_shape=jax.ShapeDtypeStruct((peers, rows, segments), f32),
        in_specs=[HBM] * 9,
        out_specs=HBM,
        scratch_shapes=[pltpu.VMEM(x.shape, x.dtype) for x in operands]
        + [pltpu.VMEM((peers, rows, segments), f32), pltpu.SemaphoreType.DMA((9,)), pltpu.SemaphoreType.DMA((4,))],
    )(*operands)
    got = lax.all_to_all(sent, EXCHANGE, split_axis=0, concat_axis=0, tiled=True)
    count = lax.axis_size("elem")
    before = lax.ppermute(place[:, -1:], "elem", [(i, i + 1) for i in range(count - 1)])
    after = lax.ppermute(place[:, :1], "elem", [(i + 1, i) for i in range(count - 1)])
    shape = jax.ShapeDtypeStruct
    kept = pl.pallas_call(
        functools.partial(window_kernel, order),
        out_shape=[
            shape((peers, rows + 2 * slots, segments), f32),
            shape((2 * patches, 2 * slots * peers), bf16),
            shape((nodes, 2 * segments), bf16),
            shape((nodes, 2 * segments), bf16),
            shape((3, patches, nodes), f32),
            shape((patches, nodes), f32),
        ],
        in_specs=[VMEM] * 11,
        out_specs=[VMEM] * 6,
        compiler_params=SMALL,
        cost_estimate=pl.CostEstimate(flops=6 * 3 * patches * nodes * nodes, bytes_accessed=4 * peers * rows * segments, transcendentals=0),
    )(sent, send, pair_slave, place, speed, before, after, inv_mass, stiffness, slave_shape, master_shape)
    velocity, contact = pl.pallas_call(
        force_kernel,
        out_shape=[shape((3, patches, nodes), f32)] * 2,
        in_specs=[VMEM] * 7,
        out_specs=[VMEM] * 2,
        scratch_shapes=[pltpu.VMEM((2 * slots * peers, 3 * segments), bf16)] * 2,
        compiler_params=SMALL,
    )(got, *kept)
    return jnp.transpose(velocity, (1, 0, 2)), jnp.transpose(contact, (1, 0, 2))


def solution(mesh):
    both = ("dom", "elem")
    placed = (
        P(both, None, None),
        P(both, None, None),
        P(both, None),
        P(both, None, None),
        P(both, None),
        P(both, None),
        P(both, None, None),
        P(both, None, None, None),
        P(),
        P(),
        P(),
    )
    return jax.shard_map(
        on_device,
        mesh=mesh,
        in_specs=placed,
        out_specs=(P(both, None, None), P(both, None, None)),
        check_vma=False,
    )
```

```python
import functools

import jax
import jax.numpy as jnp
from jax import lax
from jax.experimental import pallas as pl
from jax.experimental.pallas import tpu as pltpu
from jax.sharding import PartitionSpec as P

VMEM = pl.BlockSpec(memory_space=pltpu.VMEM)
HBM = pl.BlockSpec(memory_space=pltpu.HBM)
SMALL = pltpu.CompilerParams(vmem_limit_bytes=16 << 20)
BOTH = ("dom", "elem")
NN = (((1,), (0,)), ((), ()))
NT = (((1,), (1,)), ((), ()))
TN = (((0,), (0,)), ((), ()))


def dot(a, b, dims):
    return lax.dot_general(a, b, dims, preferred_element_type=jnp.float32)


def split(x):
    high = x.astype(jnp.bfloat16)
    return high, (x - high.astype(jnp.float32)).astype(jnp.bfloat16)


def dot3(a, b, dims):
    a_high, a_low = split(a)
    b_high, b_low = split(b)
    return dot(a_high, b_high, dims) + (dot(a_high, b_low, dims) + dot(a_low, b_high, dims))


def spot_in_exchange(peer):
    doms, elems = lax.axis_size("dom"), lax.axis_size("elem")
    if doms % 2 or elems % 2:
        return peer
    half = doms // 2
    dom, elem = peer // elems, peer % elems
    return (((elem // 2) * half + dom % half) * 2 + elem % 2) * 2 + (1 - dom // half)


def exchange_order():
    return sorted(range(lax.axis_size("dom") * lax.axis_size("elem")), key=spot_in_exchange)


def index_table(send, slave, patches, master_first):
    slots, peers = send.shape
    width = 2 * slots
    columns = peers * width
    pairs = peers * slots
    master_at, slave_at = (0, slots) if master_first else (slots, 0)

    def iota(shape, dim):
        return lax.broadcasted_iota(jnp.int32, shape, dim)

    column = iota((1, columns), 1)
    spot, place = column // width, column % width
    spread = (spot_in_exchange(iota((peers, 1), 0)) == spot).astype(jnp.bfloat16)
    masters = dot(send.astype(jnp.bfloat16), spread, NN)
    masters = jnp.sum(jnp.where(iota((slots, 1), 0) + master_at == place, masters, 0.0), axis=0, keepdims=True)
    pair = iota((pairs, 1), 0)
    spread = (spot_in_exchange(pair // slots) * width + slave_at + pair % slots == column).astype(jnp.bfloat16)
    slaves = dot((slave + patches).astype(jnp.bfloat16), spread, NN)
    row = (masters + slaves).astype(jnp.int32)
    return (iota((2 * patches, columns), 0) == row).astype(jnp.bfloat16)


def pack_kernel(order, *refs):
    ins, out_hbm, vmem, packed, table_ref, in_sems, out_sems = refs[:9], refs[9], refs[10:19], refs[19], refs[20], refs[21], refs[22]
    loads = [pltpu.make_async_copy(ins[i], vmem[i], in_sems.at[i]) for i in range(9)]
    for load in loads:
        load.start()
    send_ref, slave_ref, live_ref, position_ref, velocity_ref, master_ref, slave_shape_ref, normal_ref, weight_ref = vmem
    _, patches, nodes = position_ref.shape
    slots, peers = send_ref.shape
    segments = weight_ref.shape[-1]
    width = 2 * slots
    for i in (0, 1, 2):
        loads[i].wait()
    table = index_table(send_ref[...], slave_ref[...], patches, True).astype(jnp.float32)
    table = jnp.transpose(table).astype(jnp.bfloat16)
    table_ref[...] = jnp.concatenate([table, table], axis=1)
    live = live_ref[...].astype(jnp.float32).reshape(peers * slots, 1)
    for i in (3, 4, 5, 6):
        loads[i].wait()
    high, low = split((position_ref[...] + 0.5 * velocity_ref[...]).reshape(3 * patches, nodes))
    shape_high, shape_low = split(jnp.concatenate([master_ref[...], slave_shape_ref[...]], axis=1))
    projected = dot(jnp.concatenate([high, low], axis=1), jnp.concatenate([shape_high, shape_high], axis=0), NN)
    projected = (projected + dot(high, shape_low, NN)).reshape(3, patches, 2 * segments)
    loads[7].wait()
    loads[8].wait()
    weight_ref[...] = weight_ref[...] * live
    high, low = split(
        jnp.concatenate([jnp.concatenate([projected[c, :, :segments], projected[c, :, segments:]], axis=0) for c in range(3)], axis=1)
    )
    picked = dot(table_ref[...], jnp.concatenate([high, low], axis=0), NN)
    group = 8
    first = lax.broadcasted_iota(jnp.int32, (group, width, segments), 1) < slots

    def placed(load, peer, half):
        x = load(pl.ds(peer // 2 * width, width))
        x = pltpu.roll(x, slots, 0) if (peer + half) % 2 else x
        return x.reshape(1, width, segments)

    stores = []
    for g in range(0, peers, group):
        gap = jnp.zeros((group, width, segments), jnp.float32)
        for c in range(3):
            chosen = picked[g * width : (g + group) * width, c * segments : (c + 1) * segments].reshape(group, width, segments)
            normal = jnp.concatenate([placed(lambda rows: normal_ref[c, rows, :], p, 1) for p in order[g : g + group]], axis=0)
            gap = gap + normal * chosen
            packed[g : g + group, c * width : (c + 1) * width, :] = jnp.where(first, chosen, normal)
        weight = jnp.concatenate([placed(lambda rows: weight_ref[rows, :], p, 0) for p in order[g : g + group]], axis=0)
        packed[g : g + group, 3 * width : 4 * width, :] = jnp.where(first, weight, gap)
        rows = pl.ds(g, group)
        stores.append(pltpu.make_async_copy(packed.at[rows], out_hbm.at[rows], out_sems.at[g // group]))
        stores[-1].start()
    for store in stores:
        store.wait()


def window_kernel(
    sent_ref, send_ref, slave_ref, position_ref, velocity_ref, before_ref, after_ref, mass_ref, stiffness_ref, slave_shape_ref, master_shape_ref,
    own_ref, table_ref, shape_ref, base_ref, half_ref,
):
    _, patches, nodes = position_ref.shape
    slots, peers = send_ref.shape
    width = 2 * slots
    for t in range(4):
        own_ref[:, t * width : (t + 1) * width, :] = pltpu.roll(sent_ref[:, t * width : (t + 1) * width, :], slots, 1)
    own_ref[:, 4 * width :, :] = sent_ref[:, 3 * width : 4 * width, :]
    table = index_table(send_ref[...], slave_ref[...], patches, False)
    table_ref[...] = jnp.concatenate([table, table], axis=1)
    high, low = split(jnp.concatenate([-master_shape_ref[...], slave_shape_ref[...]], axis=1))
    shape_ref[...] = jnp.concatenate([high, low, high], axis=1)
    row = lax.broadcasted_iota(jnp.int32, (patches, nodes), 0)
    position = position_ref[...]
    product = dot3(position.reshape(3 * patches, nodes), stiffness_ref[...], NN).reshape(3, patches, nodes)
    half = 0.5 * mass_ref[...]
    half_ref[...] = half
    for c in range(3):
        x = position[c]
        before = jnp.where(row == 0, before_ref[c], pltpu.roll(x, 1, 0))
        after = jnp.where(row == patches - 1, after_ref[c], pltpu.roll(x, patches - 1, 0))
        internal = 0.5 * (before + after - 2.0 * x) - product[c]
        base_ref[c] = velocity_ref[c] + half * internal


def force_kernel(got_ref, own_ref, table_ref, shape_ref, base_ref, half_ref, velocity_ref, contact_ref, traction_ref):
    _, patches, nodes = base_ref.shape
    peers, _, segments = got_ref.shape
    width = got_ref.shape[1] // 4
    slots = width // 2
    entries = peers * width
    group = 8

    def tile(ref, g, t):
        return ref[g : g + group, t * width : (t + 1) * width, :]

    first = lax.broadcasted_iota(jnp.int32, (group, width, segments), 1) < slots
    for g in range(0, peers, group):
        last = tile(got_ref, g, 3)
        gap = jnp.where(first, tile(own_ref, g, 3), last)
        for c in range(3):
            gap = gap - tile(got_ref, g, c) * tile(own_ref, g, c)
        weight = jnp.where(first, tile(own_ref, g, 4), pltpu.roll(last, slots, 1))
        pressure = (jnp.maximum(-gap, 0.0) + jnp.log1p(jnp.exp(-jnp.abs(gap)))) * weight
        for c in range(3):
            normal = jnp.where(first, tile(own_ref, g, c), tile(got_ref, g, c))
            high, low = split((normal * pressure).reshape(group * width, segments))
            for at, part in ((0, high), (entries, low)):
                traction_ref[at + g * width : at + (g + group) * width, c * segments : (c + 1) * segments] = part
    summed = dot(table_ref[...], traction_ref[...], NN)
    summed = jnp.concatenate(
        [
            jnp.concatenate([summed[:patches, c * segments : (c + 1) * segments], summed[patches:, c * segments : (c + 1) * segments]], axis=1)
            for c in range(3)
        ],
        axis=0,
    )
    high, low = split(summed)
    contact = dot(jnp.concatenate([high, high, low], axis=1), shape_ref[...], NT).reshape(3, patches, nodes)
    contact_ref[...] = contact
    velocity_ref[...] = base_ref[...] + half_ref[...] * contact


def on_device(
    positions,
    velocities,
    inv_mass,
    send_index,
    pair_slave,
    pair_live,
    quad_weights,
    seg_normals,
    slave_shape,
    master_shape,
    stiffness,
):
    patches, _, nodes = positions.shape
    _, peers, slots = send_index.shape
    segments = quad_weights.shape[-1]
    rows = 8 * slots
    f32, bf16 = jnp.float32, jnp.bfloat16
    order = exchange_order()
    place = jnp.transpose(positions, (1, 0, 2))
    speed = jnp.transpose(velocities, (1, 0, 2))
    send = jnp.transpose(send_index[0], (1, 0))
    normals = jnp.transpose(seg_normals[0], (1, 0, 2))
    operands = (send, pair_slave, pair_live, place, speed, master_shape, slave_shape, normals, quad_weights[0])
    sent = pl.pallas_call(
        functools.partial(pack_kernel, order),
        out_shape=jax.ShapeDtypeStruct((peers, rows, segments), f32),
        in_specs=[HBM] * 9,
        out_specs=HBM,
        scratch_shapes=[pltpu.VMEM(x.shape, x.dtype) for x in operands]
        + [
            pltpu.VMEM((peers, rows, segments), f32),
            pltpu.VMEM((2 * slots * peers, 4 * patches), bf16),
            pltpu.SemaphoreType.DMA((9,)),
            pltpu.SemaphoreType.DMA((peers // 8,)),
        ],
    )(*operands)
    got = lax.all_to_all(sent, BOTH, split_axis=0, concat_axis=0, tiled=True, axis_index_groups=[order])
    count = lax.axis_size("elem")
    before = lax.ppermute(place[:, -1:], "elem", [(i, i + 1) for i in range(count - 1)])
    after = lax.ppermute(place[:, :1], "elem", [(i + 1, i) for i in range(count - 1)])
    shape = jax.ShapeDtypeStruct
    kept = pl.pallas_call(
        window_kernel,
        out_shape=[
            shape((peers, rows + 2 * slots, segments), f32),
            shape((2 * patches, 4 * slots * peers), bf16),
            shape((nodes, 6 * segments), bf16),
            shape((3, patches, nodes), f32),
            shape((patches, nodes), f32),
        ],
        in_specs=[VMEM] * 11,
        out_specs=[VMEM] * 5,
        compiler_params=SMALL,
        cost_estimate=pl.CostEstimate(flops=6 * 3 * patches * nodes * nodes, bytes_accessed=4 * peers * rows * segments, transcendentals=0),
    )(sent, send, pair_slave, place, speed, before, after, inv_mass, stiffness, slave_shape, master_shape)
    velocity, contact = pl.pallas_call(
        force_kernel,
        out_shape=[shape((3, patches, nodes), f32)] * 2,
        in_specs=[VMEM] * 6,
        out_specs=[VMEM] * 2,
        scratch_shapes=[pltpu.VMEM((4 * slots * peers, 3 * segments), bf16)],
        compiler_params=SMALL,
    )(got, *kept)
    return jnp.transpose(velocity, (1, 0, 2)), jnp.transpose(contact, (1, 0, 2))


def solution(mesh):
    both = ("dom", "elem")
    placed = (
        P(both, None, None),
        P(both, None, None),
        P(both, None),
        P(both, None, None),
        P(both, None),
        P(both, None),
        P(both, None, None),
        P(both, None, None, None),
        P(),
        P(),
        P(),
    )
    return jax.shard_map(
        on_device,
        mesh=mesh,
        in_specs=placed,
        out_specs=(P(both, None, None), P(both, None, None)),
        check_vma=False,
    )
```

```python
import functools

import jax
import jax.numpy as jnp
from jax import lax
from jax.experimental import pallas as pl
from jax.experimental.pallas import tpu as pltpu
from jax.sharding import PartitionSpec as P

VMEM = pl.BlockSpec(memory_space=pltpu.VMEM)
HBM = pl.BlockSpec(memory_space=pltpu.HBM)
SMALL = pltpu.CompilerParams(vmem_limit_bytes=16 << 20)
BOTH = ("dom", "elem")
NN = (((1,), (0,)), ((), ()))
NT = (((1,), (1,)), ((), ()))
TN = (((0,), (0,)), ((), ()))


def dot(a, b, dims):
    return lax.dot_general(a, b, dims, preferred_element_type=jnp.float32)


def split(x):
    high = x.astype(jnp.bfloat16)
    return high, (x - high.astype(jnp.float32)).astype(jnp.bfloat16)


def dot3(a, b, dims):
    a_high, a_low = split(a)
    b_high, b_low = split(b)
    return dot(a_high, b_high, dims) + (dot(a_high, b_low, dims) + dot(a_low, b_high, dims))


def spot_in_exchange(peer):
    doms, elems = lax.axis_size("dom"), lax.axis_size("elem")
    if doms % 2 or elems % 2:
        return peer
    last = doms * elems - 1
    peer = peer + (peer == 1) * (last - 1) - (peer == last) * (last - 1)
    half = doms // 2
    dom, elem = peer // elems, peer % elems
    return (((elem // 2) * half + dom % half) * 2 + elem % 2) * 2 + (1 - dom // half)


def exchange_order():
    return sorted(range(lax.axis_size("dom") * lax.axis_size("elem")), key=spot_in_exchange)


def index_table(send, slave, patches, master_first):
    slots, peers = send.shape
    width = 2 * slots
    columns = peers * width
    pairs = peers * slots
    master_at, slave_at = (0, slots) if master_first else (slots, 0)

    def iota(shape, dim):
        return lax.broadcasted_iota(jnp.int32, shape, dim)

    column = iota((1, columns), 1)
    spot, place = column // width, column % width
    spread = (spot_in_exchange(iota((peers, 1), 0)) == spot).astype(jnp.bfloat16)
    masters = dot(send.astype(jnp.bfloat16), spread, NN)
    masters = jnp.sum(jnp.where(iota((slots, 1), 0) + master_at == place, masters, 0.0), axis=0, keepdims=True)
    pair = iota((pairs, 1), 0)
    spread = (spot_in_exchange(pair // slots) * width + slave_at + pair % slots == column).astype(jnp.bfloat16)
    slaves = dot((slave + patches).astype(jnp.bfloat16), spread, NN)
    row = (masters + slaves).astype(jnp.int32)
    return (iota((2 * patches, columns), 0) == row).astype(jnp.bfloat16)


def pack_kernel(order, *refs):
    ins, out_hbm, vmem, packed, table_ref, in_sems, out_sems = refs[:9], refs[9], refs[10:19], refs[19], refs[20], refs[21], refs[22]
    loads = [pltpu.make_async_copy(ins[i], vmem[i], in_sems.at[i]) for i in range(9)]
    for load in loads:
        load.start()
    send_ref, slave_ref, live_ref, position_ref, velocity_ref, master_ref, slave_shape_ref, normal_ref, weight_ref = vmem
    _, patches, nodes = position_ref.shape
    slots, peers = send_ref.shape
    segments = weight_ref.shape[-1]
    width = 2 * slots
    for i in (0, 1, 2):
        loads[i].wait()
    table = index_table(send_ref[...], slave_ref[...], patches, True).astype(jnp.float32)
    table = jnp.transpose(table).astype(jnp.bfloat16)
    table_ref[...] = jnp.concatenate([table, table], axis=1)
    live = live_ref[...].astype(jnp.float32).reshape(peers * slots, 1)
    for i in (3, 4, 5, 6):
        loads[i].wait()
    high, low = split((position_ref[...] + 0.5 * velocity_ref[...]).reshape(3 * patches, nodes))
    shape_high, shape_low = split(jnp.concatenate([master_ref[...], slave_shape_ref[...]], axis=1))
    projected = dot(jnp.concatenate([high, low], axis=1), jnp.concatenate([shape_high, shape_high], axis=0), NN)
    projected = (projected + dot(high, shape_low, NN)).reshape(3, patches, 2 * segments)
    loads[7].wait()
    loads[8].wait()
    weight_ref[...] = weight_ref[...] * live
    high, low = split(
        jnp.concatenate([jnp.concatenate([projected[c, :, :segments], projected[c, :, segments:]], axis=0) for c in range(3)], axis=1)
    )
    picked = dot(table_ref[...], jnp.concatenate([high, low], axis=0), NN)
    group = 8
    first = lax.broadcasted_iota(jnp.int32, (group, width, segments), 1) < slots

    def placed(load, peer, half):
        x = load(pl.ds(peer // 2 * width, width))
        x = pltpu.roll(x, slots, 0) if (peer + half) % 2 else x
        return x.reshape(1, width, segments)

    stores = []
    for g in range(0, peers, group):
        gap = jnp.zeros((group, width, segments), jnp.float32)
        for c in range(3):
            chosen = picked[g * width : (g + group) * width, c * segments : (c + 1) * segments].reshape(group, width, segments)
            normal = jnp.concatenate([placed(lambda rows: normal_ref[c, rows, :], p, 1) for p in order[g : g + group]], axis=0)
            gap = gap + normal * chosen
            packed[g : g + group, c * width : (c + 1) * width, :] = jnp.where(first, chosen, normal)
        weight = jnp.concatenate([placed(lambda rows: weight_ref[rows, :], p, 0) for p in order[g : g + group]], axis=0)
        packed[g : g + group, 3 * width : 4 * width, :] = jnp.where(first, weight, gap)
        rows = pl.ds(g, group)
        stores.append(pltpu.make_async_copy(packed.at[rows], out_hbm.at[rows], out_sems.at[g // group]))
        stores[-1].start()
    for store in stores:
        store.wait()


def window_kernel(
    sent_ref, send_ref, slave_ref, position_ref, velocity_ref, before_ref, after_ref, mass_ref, stiffness_ref, slave_shape_ref, master_shape_ref,
    own_ref, table_ref, shape_ref, base_ref, half_ref,
):
    _, patches, nodes = position_ref.shape
    slots, peers = send_ref.shape
    width = 2 * slots
    for t in range(4):
        own_ref[:, t * width : (t + 1) * width, :] = pltpu.roll(sent_ref[:, t * width : (t + 1) * width, :], slots, 1)
    own_ref[:, 4 * width :, :] = sent_ref[:, 3 * width : 4 * width, :]
    table = index_table(send_ref[...], slave_ref[...], patches, False)
    table_ref[...] = jnp.concatenate([table, table], axis=1)
    high, low = split(jnp.concatenate([-master_shape_ref[...], slave_shape_ref[...]], axis=1))
    shape_ref[...] = jnp.concatenate([high, low, high], axis=1)
    row = lax.broadcasted_iota(jnp.int32, (patches, nodes), 0)
    position = position_ref[...]
    product = dot3(position.reshape(3 * patches, nodes), stiffness_ref[...], NN).reshape(3, patches, nodes)
    half = 0.5 * mass_ref[...]
    half_ref[...] = half
    for c in range(3):
        x = position[c]
        before = jnp.where(row == 0, before_ref[c], pltpu.roll(x, 1, 0))
        after = jnp.where(row == patches - 1, after_ref[c], pltpu.roll(x, patches - 1, 0))
        internal = 0.5 * (before + after - 2.0 * x) - product[c]
        base_ref[c] = velocity_ref[c] + half * internal


def force_kernel(got_ref, own_ref, table_ref, shape_ref, base_ref, half_ref, velocity_ref, contact_ref, traction_ref):
    _, patches, nodes = base_ref.shape
    peers, _, segments = got_ref.shape
    width = got_ref.shape[1] // 4
    slots = width // 2
    entries = peers * width
    group = 8

    def tile(ref, g, t):
        return ref[g : g + group, t * width : (t + 1) * width, :]

    first = lax.broadcasted_iota(jnp.int32, (group, width, segments), 1) < slots
    for g in range(0, peers, group):
        last = tile(got_ref, g, 3)
        gap = jnp.where(first, tile(own_ref, g, 3), last)
        for c in range(3):
            gap = gap - tile(got_ref, g, c) * tile(own_ref, g, c)
        weight = jnp.where(first, tile(own_ref, g, 4), pltpu.roll(last, slots, 1))
        pressure = (jnp.maximum(-gap, 0.0) + jnp.log1p(jnp.exp(-jnp.abs(gap)))) * weight
        for c in range(3):
            normal = jnp.where(first, tile(own_ref, g, c), tile(got_ref, g, c))
            high, low = split((normal * pressure).reshape(group * width, segments))
            for at, part in ((0, high), (entries, low)):
                traction_ref[at + g * width : at + (g + group) * width, c * segments : (c + 1) * segments] = part
    summed = dot(table_ref[...], traction_ref[...], NN)
    summed = jnp.concatenate(
        [
            jnp.concatenate([summed[:patches, c * segments : (c + 1) * segments], summed[patches:, c * segments : (c + 1) * segments]], axis=1)
            for c in range(3)
        ],
        axis=0,
    )
    high, low = split(summed)
    contact = dot(jnp.concatenate([high, high, low], axis=1), shape_ref[...], NT).reshape(3, patches, nodes)
    contact_ref[...] = contact
    velocity_ref[...] = base_ref[...] + half_ref[...] * contact


def on_device(
    positions,
    velocities,
    inv_mass,
    send_index,
    pair_slave,
    pair_live,
    quad_weights,
    seg_normals,
    slave_shape,
    master_shape,
    stiffness,
):
    patches, _, nodes = positions.shape
    _, peers, slots = send_index.shape
    segments = quad_weights.shape[-1]
    rows = 8 * slots
    f32, bf16 = jnp.float32, jnp.bfloat16
    order = exchange_order()
    place = jnp.transpose(positions, (1, 0, 2))
    speed = jnp.transpose(velocities, (1, 0, 2))
    send = jnp.transpose(send_index[0], (1, 0))
    normals = jnp.transpose(seg_normals[0], (1, 0, 2))
    operands = (send, pair_slave, pair_live, place, speed, master_shape, slave_shape, normals, quad_weights[0])
    sent = pl.pallas_call(
        functools.partial(pack_kernel, order),
        out_shape=jax.ShapeDtypeStruct((peers, rows, segments), f32),
        in_specs=[HBM] * 9,
        out_specs=HBM,
        scratch_shapes=[pltpu.VMEM(x.shape, x.dtype) for x in operands]
        + [
            pltpu.VMEM((peers, rows, segments), f32),
            pltpu.VMEM((2 * slots * peers, 4 * patches), bf16),
            pltpu.SemaphoreType.DMA((9,)),
            pltpu.SemaphoreType.DMA((peers // 8,)),
        ],
    )(*operands)
    got = lax.all_to_all(sent, BOTH, split_axis=0, concat_axis=0, tiled=True, axis_index_groups=[order])
    count = lax.axis_size("elem")
    before = lax.ppermute(place[:, -1:], "elem", [(i, i + 1) for i in range(count - 1)])
    after = lax.ppermute(place[:, :1], "elem", [(i + 1, i) for i in range(count - 1)])
    shape = jax.ShapeDtypeStruct
    kept = pl.pallas_call(
        window_kernel,
        out_shape=[
            shape((peers, rows + 2 * slots, segments), f32),
            shape((2 * patches, 4 * slots * peers), bf16),
            shape((nodes, 6 * segments), bf16),
            shape((3, patches, nodes), f32),
            shape((patches, nodes), f32),
        ],
        in_specs=[VMEM] * 11,
        out_specs=[VMEM] * 5,
        compiler_params=SMALL,
        cost_estimate=pl.CostEstimate(flops=6 * 3 * patches * nodes * nodes, bytes_accessed=4 * peers * rows * segments, transcendentals=0),
    )(sent, send, pair_slave, place, speed, before, after, inv_mass, stiffness, slave_shape, master_shape)
    velocity, contact = pl.pallas_call(
        force_kernel,
        out_shape=[shape((3, patches, nodes), f32)] * 2,
        in_specs=[VMEM] * 6,
        out_specs=[VMEM] * 2,
        scratch_shapes=[pltpu.VMEM((4 * slots * peers, 3 * segments), bf16)],
        compiler_params=SMALL,
    )(got, *kept)
    return jnp.transpose(velocity, (1, 0, 2)), jnp.transpose(contact, (1, 0, 2))


def solution(mesh):
    both = ("dom", "elem")
    placed = (
        P(both, None, None),
        P(both, None, None),
        P(both, None),
        P(both, None, None),
        P(both, None),
        P(both, None),
        P(both, None, None),
        P(both, None, None, None),
        P(),
        P(),
        P(),
    )
    return jax.shard_map(
        on_device,
        mesh=mesh,
        in_specs=placed,
        out_specs=(P(both, None, None), P(both, None, None)),
        check_vma=False,
    )
```

```python
import functools

import jax
import jax.numpy as jnp
from jax import lax
from jax.experimental import pallas as pl
from jax.experimental.pallas import tpu as pltpu
from jax.sharding import PartitionSpec as P

VMEM = pl.BlockSpec(memory_space=pltpu.VMEM)
HBM = pl.BlockSpec(memory_space=pltpu.HBM)
SMALL = pltpu.CompilerParams(vmem_limit_bytes=16 << 20)
BOTH = ("dom", "elem")
NN = (((1,), (0,)), ((), ()))
NT = (((1,), (1,)), ((), ()))
TN = (((0,), (0,)), ((), ()))


def dot(a, b, dims):
    return lax.dot_general(a, b, dims, preferred_element_type=jnp.float32)


def split(x):
    high = x.astype(jnp.bfloat16)
    return high, (x - high.astype(jnp.float32)).astype(jnp.bfloat16)


def dot3(a, b, dims):
    a_high, a_low = split(a)
    b_high, b_low = split(b)
    return dot(a_high, b_high, dims) + (dot(a_high, b_low, dims) + dot(a_low, b_high, dims))


def spot_in_exchange(peer):
    doms, elems = lax.axis_size("dom"), lax.axis_size("elem")
    if doms % 2 or elems % 2:
        return peer
    last = doms * elems - 1
    for a, b in ((1, last), (elems, last - 1)):
        peer = peer + (peer == a) * (b - a) + (peer == b) * (a - b)
    half = doms // 2
    dom, elem = peer // elems, peer % elems
    return (((elem // 2) * half + dom % half) * 2 + elem % 2) * 2 + (1 - dom // half)


def exchange_order():
    return sorted(range(lax.axis_size("dom") * lax.axis_size("elem")), key=spot_in_exchange)


def index_table(send, slave, patches, master_first):
    slots, peers = send.shape
    width = 2 * slots
    columns = peers * width
    pairs = peers * slots
    master_at, slave_at = (0, slots) if master_first else (slots, 0)

    def iota(shape, dim):
        return lax.broadcasted_iota(jnp.int32, shape, dim)

    column = iota((1, columns), 1)
    spot, place = column // width, column % width
    spread = (spot_in_exchange(iota((peers, 1), 0)) == spot).astype(jnp.bfloat16)
    masters = dot(send.astype(jnp.bfloat16), spread, NN)
    masters = jnp.sum(jnp.where(iota((slots, 1), 0) + master_at == place, masters, 0.0), axis=0, keepdims=True)
    pair = iota((pairs, 1), 0)
    spread = (spot_in_exchange(pair // slots) * width + slave_at + pair % slots == column).astype(jnp.bfloat16)
    slaves = dot((slave + patches).astype(jnp.bfloat16), spread, NN)
    row = (masters + slaves).astype(jnp.int32)
    return (iota((2 * patches, columns), 0) == row).astype(jnp.bfloat16)


def pack_kernel(order, *refs):
    ins, out_hbm, vmem, packed, table_ref, in_sems, out_sems = refs[:9], refs[9], refs[10:19], refs[19], refs[20], refs[21], refs[22]
    loads = [pltpu.make_async_copy(ins[i], vmem[i], in_sems.at[i]) for i in range(9)]
    for load in loads:
        load.start()
    send_ref, slave_ref, live_ref, position_ref, velocity_ref, master_ref, slave_shape_ref, normal_ref, weight_ref = vmem
    _, patches, nodes = position_ref.shape
    slots, peers = send_ref.shape
    segments = weight_ref.shape[-1]
    width = 2 * slots
    for i in (0, 1, 2):
        loads[i].wait()
    table = index_table(send_ref[...], slave_ref[...], patches, True).astype(jnp.float32)
    table = jnp.transpose(table).astype(jnp.bfloat16)
    table_ref[...] = jnp.concatenate([table, table], axis=1)
    live = live_ref[...].astype(jnp.float32).reshape(peers * slots, 1)
    for i in (3, 4, 5, 6):
        loads[i].wait()
    high, low = split((position_ref[...] + 0.5 * velocity_ref[...]).reshape(3 * patches, nodes))
    shape_high, shape_low = split(jnp.concatenate([master_ref[...], slave_shape_ref[...]], axis=1))
    projected = dot(jnp.concatenate([high, low], axis=1), jnp.concatenate([shape_high, shape_high], axis=0), NN)
    projected = (projected + dot(high, shape_low, NN)).reshape(3, patches, 2 * segments)
    loads[7].wait()
    loads[8].wait()
    weight_ref[...] = weight_ref[...] * live
    high, low = split(
        jnp.concatenate([jnp.concatenate([projected[c, :, :segments], projected[c, :, segments:]], axis=0) for c in range(3)], axis=1)
    )
    picked = dot(table_ref[...], jnp.concatenate([high, low], axis=0), NN)
    group = 8
    first = lax.broadcasted_iota(jnp.int32, (group, width, segments), 1) < slots

    def placed(load, peer, half):
        x = load(pl.ds(peer // 2 * width, width))
        x = pltpu.roll(x, slots, 0) if (peer + half) % 2 else x
        return x.reshape(1, width, segments)

    stores = []
    for g in range(0, peers, group):
        gap = jnp.zeros((group, width, segments), jnp.float32)
        for c in range(3):
            chosen = picked[g * width : (g + group) * width, c * segments : (c + 1) * segments].reshape(group, width, segments)
            normal = jnp.concatenate([placed(lambda rows: normal_ref[c, rows, :], p, 1) for p in order[g : g + group]], axis=0)
            gap = gap + normal * chosen
            packed[g : g + group, c * width : (c + 1) * width, :] = jnp.where(first, chosen, normal)
        weight = jnp.concatenate([placed(lambda rows: weight_ref[rows, :], p, 0) for p in order[g : g + group]], axis=0)
        packed[g : g + group, 3 * width : 4 * width, :] = jnp.where(first, weight, gap)
        rows = pl.ds(g, group)
        stores.append(pltpu.make_async_copy(packed.at[rows], out_hbm.at[rows], out_sems.at[g // group]))
        stores[-1].start()
    for store in stores:
        store.wait()


def window_kernel(
    sent_ref, send_ref, slave_ref, position_ref, velocity_ref, before_ref, after_ref, mass_ref, stiffness_ref, slave_shape_ref, master_shape_ref,
    own_ref, table_ref, shape_ref, base_ref, half_ref,
):
    _, patches, nodes = position_ref.shape
    slots, peers = send_ref.shape
    width = 2 * slots
    for t in range(4):
        own_ref[:, t * width : (t + 1) * width, :] = pltpu.roll(sent_ref[:, t * width : (t + 1) * width, :], slots, 1)
    own_ref[:, 4 * width :, :] = sent_ref[:, 3 * width : 4 * width, :]
    table = index_table(send_ref[...], slave_ref[...], patches, False)
    table_ref[...] = jnp.concatenate([table, table], axis=1)
    high, low = split(jnp.concatenate([-master_shape_ref[...], slave_shape_ref[...]], axis=1))
    shape_ref[...] = jnp.concatenate([high, low, high], axis=1)
    row = lax.broadcasted_iota(jnp.int32, (patches, nodes), 0)
    position = position_ref[...]
    product = dot3(position.reshape(3 * patches, nodes), stiffness_ref[...], NN).reshape(3, patches, nodes)
    half = 0.5 * mass_ref[...]
    half_ref[...] = half
    for c in range(3):
        x = position[c]
        before = jnp.where(row == 0, before_ref[c], pltpu.roll(x, 1, 0))
        after = jnp.where(row == patches - 1, after_ref[c], pltpu.roll(x, patches - 1, 0))
        internal = 0.5 * (before + after - 2.0 * x) - product[c]
        base_ref[c] = velocity_ref[c] + half * internal


def force_kernel(got_ref, own_ref, table_ref, shape_ref, base_ref, half_ref, velocity_ref, contact_ref, traction_ref):
    _, patches, nodes = base_ref.shape
    peers, _, segments = got_ref.shape
    width = got_ref.shape[1] // 4
    slots = width // 2
    entries = peers * width
    group = 8

    def tile(ref, g, t):
        return ref[g : g + group, t * width : (t + 1) * width, :]

    first = lax.broadcasted_iota(jnp.int32, (group, width, segments), 1) < slots
    for g in range(0, peers, group):
        last = tile(got_ref, g, 3)
        gap = jnp.where(first, tile(own_ref, g, 3), last)
        for c in range(3):
            gap = gap - tile(got_ref, g, c) * tile(own_ref, g, c)
        weight = jnp.where(first, tile(own_ref, g, 4), pltpu.roll(last, slots, 1))
        pressure = (jnp.maximum(-gap, 0.0) + jnp.log1p(jnp.exp(-jnp.abs(gap)))) * weight
        for c in range(3):
            normal = jnp.where(first, tile(own_ref, g, c), tile(got_ref, g, c))
            high, low = split((normal * pressure).reshape(group * width, segments))
            for at, part in ((0, high), (entries, low)):
                traction_ref[at + g * width : at + (g + group) * width, c * segments : (c + 1) * segments] = part
    summed = dot(table_ref[...], traction_ref[...], NN)
    summed = jnp.concatenate(
        [
            jnp.concatenate([summed[:patches, c * segments : (c + 1) * segments], summed[patches:, c * segments : (c + 1) * segments]], axis=1)
            for c in range(3)
        ],
        axis=0,
    )
    high, low = split(summed)
    contact = dot(jnp.concatenate([high, high, low], axis=1), shape_ref[...], NT).reshape(3, patches, nodes)
    contact_ref[...] = contact
    velocity_ref[...] = base_ref[...] + half_ref[...] * contact


def on_device(
    positions,
    velocities,
    inv_mass,
    send_index,
    pair_slave,
    pair_live,
    quad_weights,
    seg_normals,
    slave_shape,
    master_shape,
    stiffness,
):
    patches, _, nodes = positions.shape
    _, peers, slots = send_index.shape
    segments = quad_weights.shape[-1]
    rows = 8 * slots
    f32, bf16 = jnp.float32, jnp.bfloat16
    order = exchange_order()
    place = jnp.transpose(positions, (1, 0, 2))
    speed = jnp.transpose(velocities, (1, 0, 2))
    send = jnp.transpose(send_index[0], (1, 0))
    normals = jnp.transpose(seg_normals[0], (1, 0, 2))
    operands = (send, pair_slave, pair_live, place, speed, master_shape, slave_shape, normals, quad_weights[0])
    sent = pl.pallas_call(
        functools.partial(pack_kernel, order),
        out_shape=jax.ShapeDtypeStruct((peers, rows, segments), f32),
        in_specs=[HBM] * 9,
        out_specs=HBM,
        scratch_shapes=[pltpu.VMEM(x.shape, x.dtype) for x in operands]
        + [
            pltpu.VMEM((peers, rows, segments), f32),
            pltpu.VMEM((2 * slots * peers, 4 * patches), bf16),
            pltpu.SemaphoreType.DMA((9,)),
            pltpu.SemaphoreType.DMA((peers // 8,)),
        ],
    )(*operands)
    got = lax.all_to_all(sent, BOTH, split_axis=0, concat_axis=0, tiled=True, axis_index_groups=[order])
    count = lax.axis_size("elem")
    before = lax.ppermute(place[:, -1:], "elem", [(i, i + 1) for i in range(count - 1)])
    after = lax.ppermute(place[:, :1], "elem", [(i + 1, i) for i in range(count - 1)])
    shape = jax.ShapeDtypeStruct
    kept = pl.pallas_call(
        window_kernel,
        out_shape=[
            shape((peers, rows + 2 * slots, segments), f32),
            shape((2 * patches, 4 * slots * peers), bf16),
            shape((nodes, 6 * segments), bf16),
            shape((3, patches, nodes), f32),
            shape((patches, nodes), f32),
        ],
        in_specs=[VMEM] * 11,
        out_specs=[VMEM] * 5,
        compiler_params=SMALL,
        cost_estimate=pl.CostEstimate(flops=6 * 3 * patches * nodes * nodes, bytes_accessed=4 * peers * rows * segments, transcendentals=0),
    )(sent, send, pair_slave, place, speed, before, after, inv_mass, stiffness, slave_shape, master_shape)
    velocity, contact = pl.pallas_call(
        force_kernel,
        out_shape=[shape((3, patches, nodes), f32)] * 2,
        in_specs=[VMEM] * 6,
        out_specs=[VMEM] * 2,
        scratch_shapes=[pltpu.VMEM((4 * slots * peers, 3 * segments), bf16)],
        compiler_params=SMALL,
    )(got, *kept)
    return jnp.transpose(velocity, (1, 0, 2)), jnp.transpose(contact, (1, 0, 2))


def solution(mesh):
    both = ("dom", "elem")
    placed = (
        P(both, None, None),
        P(both, None, None),
        P(both, None),
        P(both, None, None),
        P(both, None),
        P(both, None),
        P(both, None, None),
        P(both, None, None, None),
        P(),
        P(),
        P(),
    )
    return jax.shard_map(
        on_device,
        mesh=mesh,
        in_specs=placed,
        out_specs=(P(both, None, None), P(both, None, None)),
        check_vma=False,
    )
```

```python
import functools

import jax
import jax.numpy as jnp
from jax import lax
from jax.experimental import pallas as pl
from jax.experimental.pallas import tpu as pltpu
from jax.sharding import PartitionSpec as P

VMEM = pl.BlockSpec(memory_space=pltpu.VMEM)
HBM = pl.BlockSpec(memory_space=pltpu.HBM)
SMALL = pltpu.CompilerParams(vmem_limit_bytes=16 << 20)
BOTH = ("dom", "elem")
NN = (((1,), (0,)), ((), ()))
NT = (((1,), (1,)), ((), ()))
TN = (((0,), (0,)), ((), ()))


def dot(a, b, dims):
    return lax.dot_general(a, b, dims, preferred_element_type=jnp.float32)


def split(x):
    high = x.astype(jnp.bfloat16)
    return high, (x - high.astype(jnp.float32)).astype(jnp.bfloat16)


def dot3(a, b, dims):
    a_high, a_low = split(a)
    b_high, b_low = split(b)
    return dot(a_high, b_high, dims) + (dot(a_high, b_low, dims) + dot(a_low, b_high, dims))


def spot_in_exchange(peer):
    doms, elems = lax.axis_size("dom"), lax.axis_size("elem")
    if doms % 2 or elems % 2:
        return peer
    last = doms * elems - 1
    for a, b in ((1, last), (elems, last - 1)):
        peer = peer + (peer == a) * (b - a) + (peer == b) * (a - b)
    half = doms // 2
    dom, elem = peer // elems, peer % elems
    return (((elem // 2) * half + dom % half) * 2 + elem % 2) * 2 + (1 - dom // half)


def exchange_order():
    return sorted(range(lax.axis_size("dom") * lax.axis_size("elem")), key=spot_in_exchange)


def index_table(send, slave, patches, master_first):
    slots, peers = send.shape
    width = 2 * slots
    columns = peers * width
    pairs = peers * slots
    master_at, slave_at = (0, slots) if master_first else (slots, 0)

    def iota(shape, dim):
        return lax.broadcasted_iota(jnp.int32, shape, dim)

    column = iota((1, columns), 1)
    spot, place = column // width, column % width
    spread = (spot_in_exchange(iota((peers, 1), 0)) == spot).astype(jnp.bfloat16)
    masters = dot(send.astype(jnp.bfloat16), spread, NN)
    masters = jnp.sum(jnp.where(iota((slots, 1), 0) + master_at == place, masters, 0.0), axis=0, keepdims=True)
    pair = iota((pairs, 1), 0)
    spread = (spot_in_exchange(pair // slots) * width + slave_at + pair % slots == column).astype(jnp.bfloat16)
    slaves = dot((slave + patches).astype(jnp.bfloat16), spread, NN)
    row = (masters + slaves).astype(jnp.int32)
    return (iota((2 * patches, columns), 0) == row).astype(jnp.bfloat16)


def pack_kernel(order, *refs):
    ins, out_hbm, vmem, packed, table_ref, in_sems, out_sems = refs[:9], refs[9], refs[10:19], refs[19], refs[20], refs[21], refs[22]
    loads = [pltpu.make_async_copy(ins[i], vmem[i], in_sems.at[i]) for i in range(9)]
    for load in loads:
        load.start()
    send_ref, slave_ref, live_ref, position_ref, velocity_ref, master_ref, slave_shape_ref, normal_ref, weight_ref = vmem
    _, patches, nodes = position_ref.shape
    slots, peers = send_ref.shape
    segments = weight_ref.shape[-1]
    width = 2 * slots
    for i in (0, 1, 2):
        loads[i].wait()
    table = index_table(send_ref[...], slave_ref[...], patches, True).astype(jnp.float32)
    table = jnp.transpose(table).astype(jnp.bfloat16)
    table_ref[...] = jnp.concatenate([table, table], axis=1)
    live = live_ref[...].astype(jnp.float32).reshape(peers * slots, 1)
    for i in (3, 4, 5, 6):
        loads[i].wait()
    high, low = split((position_ref[...] + 0.5 * velocity_ref[...]).reshape(3 * patches, nodes))
    shape_high, shape_low = split(jnp.concatenate([master_ref[...], slave_shape_ref[...]], axis=1))
    projected = dot(jnp.concatenate([high, low], axis=1), jnp.concatenate([shape_high, shape_high], axis=0), NN)
    projected = (projected + dot(high, shape_low, NN)).reshape(3, patches, 2 * segments)
    loads[7].wait()
    loads[8].wait()
    weight_ref[...] = weight_ref[...] * live
    high, low = split(
        jnp.concatenate([jnp.concatenate([projected[c, :, :segments], projected[c, :, segments:]], axis=0) for c in range(3)], axis=1)
    )
    picked = dot(table_ref[...], jnp.concatenate([high, low], axis=0), NN)
    group = 8
    first = lax.broadcasted_iota(jnp.int32, (group, width, segments), 1) < slots

    def placed(load, peer, half):
        x = load(pl.ds(peer // 2 * width, width))
        x = pltpu.roll(x, slots, 0) if (peer + half) % 2 else x
        return x.reshape(1, width, segments)

    stores = []
    for g in range(0, peers, group):
        gap = jnp.zeros((group, width, segments), jnp.float32)
        for c in range(3):
            chosen = picked[g * width : (g + group) * width, c * segments : (c + 1) * segments].reshape(group, width, segments)
            normal = jnp.concatenate([placed(lambda rows: normal_ref[c, rows, :], p, 1) for p in order[g : g + group]], axis=0)
            gap = gap + normal * chosen
            packed[g : g + group, c * width : (c + 1) * width, :] = jnp.where(first, chosen, normal)
        weight = jnp.concatenate([placed(lambda rows: weight_ref[rows, :], p, 0) for p in order[g : g + group]], axis=0)
        packed[g : g + group, 3 * width : 4 * width, :] = jnp.where(first, weight, gap)
        rows = pl.ds(g, group)
        stores.append(pltpu.make_async_copy(packed.at[rows], out_hbm.at[rows], out_sems.at[g // group]))
        stores[-1].start()
    for store in stores:
        store.wait()


def window_kernel(
    sent_ref, send_ref, slave_ref, position_ref, velocity_ref, before_ref, after_ref, mass_ref, stiffness_ref, slave_shape_ref, master_shape_ref,
    own_ref, table_ref, shape_ref, base_ref, half_ref,
):
    _, patches, nodes = position_ref.shape
    slots, peers = send_ref.shape
    width = 2 * slots
    for t in range(4):
        own_ref[:, t * width : (t + 1) * width, :] = pltpu.roll(sent_ref[:, t * width : (t + 1) * width, :], slots, 1)
    own_ref[:, 4 * width :, :] = sent_ref[:, 3 * width : 4 * width, :]
    table = index_table(send_ref[...], slave_ref[...], patches, False)
    table_ref[...] = jnp.concatenate([table, table], axis=1)
    high, low = split(jnp.concatenate([-master_shape_ref[...], slave_shape_ref[...]], axis=1))
    shape_ref[...] = jnp.concatenate([high, low, high], axis=1)
    row = lax.broadcasted_iota(jnp.int32, (patches, nodes), 0)
    position = position_ref[...]
    product = dot3(position.reshape(3 * patches, nodes), stiffness_ref[...], NN).reshape(3, patches, nodes)
    half = 0.5 * mass_ref[...]
    half_ref[...] = half
    for c in range(3):
        x = position[c]
        before = jnp.where(row == 0, before_ref[c], pltpu.roll(x, 1, 0))
        after = jnp.where(row == patches - 1, after_ref[c], pltpu.roll(x, patches - 1, 0))
        internal = 0.5 * (before + after - 2.0 * x) - product[c]
        base_ref[c] = velocity_ref[c] + half * internal


def force_kernel(got_ref, own_ref, table_ref, shape_ref, base_ref, half_ref, velocity_ref, contact_ref, traction_ref):
    _, patches, nodes = base_ref.shape
    peers, _, segments = got_ref.shape
    width = got_ref.shape[1] // 4
    slots = width // 2
    entries = peers * width
    group = 8

    def tile(ref, g, t):
        return ref[g : g + group, t * width : (t + 1) * width, :]

    first = lax.broadcasted_iota(jnp.int32, (group, width, segments), 1) < slots
    for g in range(0, peers, group):
        last = tile(got_ref, g, 3)
        gap = jnp.where(first, tile(own_ref, g, 3), last)
        for c in range(3):
            gap = gap - tile(got_ref, g, c) * tile(own_ref, g, c)
        weight = jnp.where(first, tile(own_ref, g, 4), pltpu.roll(last, slots, 1))
        pressure = (jnp.maximum(-gap, 0.0) + jnp.log1p(jnp.exp(-jnp.abs(gap)))) * weight
        for c in range(3):
            normal = jnp.where(first, tile(own_ref, g, c), tile(got_ref, g, c))
            high, low = split((normal * pressure).reshape(group * width, segments))
            for at, part in ((0, high), (entries, low)):
                traction_ref[at + g * width : at + (g + group) * width, c * segments : (c + 1) * segments] = part
    summed = dot(table_ref[...], traction_ref[...], NN)
    summed = jnp.concatenate(
        [
            jnp.concatenate([summed[:patches, c * segments : (c + 1) * segments], summed[patches:, c * segments : (c + 1) * segments]], axis=1)
            for c in range(3)
        ],
        axis=0,
    )
    high, low = split(summed)
    contact = dot(jnp.concatenate([high, high, low], axis=1), shape_ref[...], NT).reshape(3, patches, nodes)
    contact_ref[...] = contact
    velocity_ref[...] = base_ref[...] + half_ref[...] * contact


def on_device(
    positions,
    velocities,
    inv_mass,
    send_index,
    pair_slave,
    pair_live,
    quad_weights,
    seg_normals,
    slave_shape,
    master_shape,
    stiffness,
):
    patches, _, nodes = positions.shape
    _, peers, slots = send_index.shape
    segments = quad_weights.shape[-1]
    rows = 8 * slots
    f32, bf16 = jnp.float32, jnp.bfloat16
    order = exchange_order()
    place = jnp.transpose(positions, (1, 0, 2))
    speed = jnp.transpose(velocities, (1, 0, 2))
    send = jnp.transpose(send_index[0], (1, 0))
    normals = jnp.transpose(seg_normals[0], (1, 0, 2))
    operands = (send, pair_slave, pair_live, place, speed, master_shape, slave_shape, normals, quad_weights[0])
    sent = pl.pallas_call(
        functools.partial(pack_kernel, order),
        out_shape=jax.ShapeDtypeStruct((peers, rows, segments), f32),
        in_specs=[HBM] * 9,
        out_specs=HBM,
        scratch_shapes=[pltpu.VMEM(x.shape, x.dtype) for x in operands]
        + [
            pltpu.VMEM((peers, rows, segments), f32),
            pltpu.VMEM((2 * slots * peers, 4 * patches), bf16),
            pltpu.SemaphoreType.DMA((9,)),
            pltpu.SemaphoreType.DMA((peers // 8,)),
        ],
        compiler_params=pltpu.CompilerParams(),
    )(*operands)
    got = lax.all_to_all(sent, BOTH, split_axis=0, concat_axis=0, tiled=True, axis_index_groups=[order])
    count = lax.axis_size("elem")
    before = lax.ppermute(place[:, -1:], "elem", [(i, i + 1) for i in range(count - 1)])
    after = lax.ppermute(place[:, :1], "elem", [(i + 1, i) for i in range(count - 1)])
    shape = jax.ShapeDtypeStruct
    kept = pl.pallas_call(
        window_kernel,
        out_shape=[
            shape((peers, rows + 2 * slots, segments), f32),
            shape((2 * patches, 4 * slots * peers), bf16),
            shape((nodes, 6 * segments), bf16),
            shape((3, patches, nodes), f32),
            shape((patches, nodes), f32),
        ],
        in_specs=[VMEM] * 11,
        out_specs=[VMEM] * 5,
        compiler_params=SMALL,
        cost_estimate=pl.CostEstimate(flops=6 * 3 * patches * nodes * nodes, bytes_accessed=4 * peers * rows * segments, transcendentals=0),
    )(sent, send, pair_slave, place, speed, before, after, inv_mass, stiffness, slave_shape, master_shape)
    velocity, contact = pl.pallas_call(
        force_kernel,
        out_shape=[shape((3, patches, nodes), f32)] * 2,
        in_specs=[VMEM] * 6,
        out_specs=[VMEM] * 2,
        scratch_shapes=[pltpu.VMEM((4 * slots * peers, 3 * segments), bf16)],
        compiler_params=pltpu.CompilerParams(
            vmem_limit_bytes=16 << 20
        ),
    )(got, *kept)
    return jnp.transpose(velocity, (1, 0, 2)), jnp.transpose(contact, (1, 0, 2))


def solution(mesh):
    both = ("dom", "elem")
    placed = (
        P(both, None, None),
        P(both, None, None),
        P(both, None),
        P(both, None, None),
        P(both, None),
        P(both, None),
        P(both, None, None),
        P(both, None, None, None),
        P(),
        P(),
        P(),
    )
    return jax.shard_map(
        on_device,
        mesh=mesh,
        in_specs=placed,
        out_specs=(P(both, None, None), P(both, None, None)),
        check_vma=False,
    )
```
